1024 devices in a mesh: vol: 16 (over x, core), surf: 64 (over z, y).
Axes of the slice: x: 8, y: 8, z: 8, core: 2. Of those that a mesh axis runs over, the one named last changes fastest.
Arguments:
- points: float32 [3, 131072], P(None, ('vol', 'surf')), may hold values from -1 to 1
- surface_points: float32 [3, 65536], P(None, 'surf'), may hold values from -1 to 1
- displacement: float32 [3, 65536], P(None, 'surf'), may hold values from -6 to 6
- rotation: float32 [3, 65536], P(None, 'surf'), may hold values from -3 to 3
- halo_index: int32 [32768], P(('vol', 'surf')), may hold values from 0 to 127
- connectivity: int32 [4, 524288], P(None, ('vol', 'surf')), may hold values from 0 to 191
Outputs:
- node_motion: float32 [3, 131072], P(None, ('vol', 'surf'))
- swept: float32 [524288], P(('vol', 'surf'))
The draws below stay inside these ranges and needn't reach their ends.
All inputs are finite; a program needn't handle non-finite values.
Results may differ from the reference program's by a relative error of at most 0.0003.
Values sent between devices are 32-bit elements; how exact they have to be, the bound alone decides.
No kernel may reach another device: no remote copies, remote signals or barrier semaphores. Data moves between devices by JAX's collectives and lax.ppermute only.
A program may use at most 32 MiB of HBM per device.

```python
import math
import jax
import jax.numpy as jnp
from jax import lax

VOL_DEV = 128
H_DEV = 32
CELLS_DEV = 512
NV = 131072
NS = 65536
NH = 32768
NC = 524288
DEVICES = 1024


def with_ends(result, key, low, largest):
    longest = result.shape.index(max(result.shape))
    spots = []
    for shift in (0, 1):
        where = [jax.random.randint(jax.random.fold_in(key, axis), (), 0, length) for axis, length in enumerate(result.shape)]
        where[longest] = (where[longest] + shift) % result.shape[longest]
        spots.append(tuple(where))
    return result.at[spots[0]].set(low).at[spots[1]].set(largest)


def levels(stream_key, shape, shards, low, largest):
    factor_of = 1.0
    for axis_at, blocks in shards:
        steps = jax.random.uniform(jax.random.fold_in(jax.random.fold_in(stream_key, 6), axis_at), (blocks,), jnp.float32, low / len(shards), largest / len(shards))
        factor_of = factor_of * jnp.repeat(jnp.exp(steps), shape[axis_at] // blocks).reshape((-1,) + (1,) * (len(shape) - 1 - axis_at))
    return factor_of


def centred(key, dims, deviation, most, cuts=(), kind=jnp.bfloat16):
    array = jax.random.normal(key, dims, jnp.float32) * deviation
    if len(cuts) > 0:
        array = levels(key, dims, cuts, -0.22, 0.18) * array
    return jnp.clip(array, min=-most, max=most).astype(kind)


def setup_inputs(seed: int = 0) -> dict:
    splits = jax.random.split(jax.random.key(seed), 7)
    points = jnp.clip(jax.random.uniform(splits[0], (3, NV), jnp.float32, -1.0, 1.0) * levels(splits[0], (3, NV), ((1, 1024),), -0.4, 0.0), -1.0, 1.0)
    surface_points = jnp.clip(jax.random.uniform(splits[1], (3, NS), jnp.float32, -1.0, 1.0) * levels(splits[1], (3, NS), ((1, 64),), -0.4, 0.0), -1.0, 1.0)
    displacement = centred(splits[2], (3, NS), 1.0, 6.0, ((1, 64),), jnp.float32)
    rotation = centred(splits[3], (3, NS), 0.5, 3.0, ((1, 64),), jnp.float32)
    halo_index = with_ends(jax.random.randint(splits[4], (NH,), 0, VOL_DEV), jax.random.fold_in(splits[4], 1), 0, VOL_DEV - 1).astype(jnp.int32)
    connectivity = with_ends(jax.random.randint(splits[5], (4, NC), 0, VOL_DEV + 2 * H_DEV), jax.random.fold_in(splits[5], 1), 0, (VOL_DEV + 2 * H_DEV) - 1).astype(jnp.int32)
    return dict(points=points, surface_points=surface_points, displacement=displacement, rotation=rotation, halo_index=halo_index, connectivity=connectivity)


SOFTENING = 0.01

def surface_terms(surface_points, displacement, rotation):
    rotated = jnp.cross(rotation, surface_points, axis=0)
    unit_row = jnp.ones_like(surface_points[0:1])
    return jnp.concatenate([displacement - rotated, rotation, unit_row], axis=0)

def pair_weight(node_points, anchors):
    gap_x = node_points[0][:, None] - anchors[0][None, :]
    gap_y = node_points[1][:, None] - anchors[1][None, :]
    gap_z = node_points[2][:, None] - anchors[2][None, :]
    spread = gap_x * gap_x + gap_y * gap_y + gap_z * gap_z + SOFTENING
    return lax.rsqrt(spread) / spread

def weighted_sums(node_points, anchors, term_rows):
    weight = pair_weight(node_points, anchors)
    return jnp.einsum('ns,cs->cn', weight, term_rows, precision=lax.Precision.HIGHEST)

def node_shift(node_points, totals):
    return (totals[0:3] + jnp.cross(totals[3:6], node_points, axis=0)) / totals[6:7]

def swept_volume(corners):
    initial = corners[0:3]
    motion = corners[3:6]
    halfway = initial + 0.5 * motion
    face_list = ((1, 2, 3), (0, 3, 2), (0, 1, 3), (0, 2, 1))
    swept_sum = jnp.zeros(corners.shape[2:], corners.dtype)
    for first, second, third in face_list:
        normal = 0.5 * jnp.cross(halfway[:, second] - halfway[:, first], halfway[:, third] - halfway[:, first], axis=0)
        average = (motion[:, first] + motion[:, second] + motion[:, third]) / 3.0
        swept_sum = swept_sum + lax.optimization_barrier(jnp.sum(average * normal, axis=0))
    return swept_sum

def reference(points, surface_points, displacement, rotation, halo_index, connectivity):
    term_rows = surface_terms(surface_points, displacement, rotation)
    block_size = math.gcd(NV, 512)
    block_count = NV // block_size
    blocks = points.reshape(3, block_count, block_size).transpose(1, 0, 2)
    totals = lax.map(lambda block_points: weighted_sums(block_points, surface_points, term_rows), blocks)
    totals = totals.transpose(1, 0, 2).reshape(7, NV)
    node_motion = node_shift(points, totals)
    node_state = jnp.concatenate([points, node_motion], axis=0).reshape(6, DEVICES, VOL_DEV)
    rim_index = halo_index.reshape(DEVICES, H_DEV).astype(jnp.int32)
    lent = jnp.take_along_axis(node_state, rim_index[None], axis=2)
    extended = jnp.concatenate([jnp.roll(lent, 1, axis=1), node_state, jnp.roll(lent, -1, axis=1)], axis=2)
    cell_nodes = connectivity.reshape(4, DEVICES, CELLS_DEV).astype(jnp.int32)

    def pick_corners(block_state, block_cells):
        return block_state[:, block_cells]
    corners = jax.vmap(pick_corners, in_axes=(1, 1), out_axes=2)(extended, cell_nodes)
    swept = swept_volume(corners).reshape(NC)
    return (node_motion, swept)
```

```python
import jax
import jax.numpy as jnp
from jax import lax
from jax.experimental import pallas as pl
from jax.experimental.pallas import tpu as pltpu
from jax.sharding import Mesh
from jax.sharding import PartitionSpec as P

SOFTENING = 0.01
F32 = jnp.float32
BF16 = jnp.bfloat16
SIDE = 8
LANES = 128
NODE_STEP = 384
SURF_STEP = 1024
NT = (((1,), (1,)), ((), ()))


def rows_of(shape):
    return lax.broadcasted_iota(jnp.int32, shape, 0)


def lanes_of(shape):
    return lax.broadcasted_iota(jnp.int32, shape, 1)


def cross3(a, b):
    return (
        a[1] * b[2] - a[2] * b[1],
        a[2] * b[0] - a[0] * b[2],
        a[0] * b[1] - a[1] * b[0],
    )


def in_three(value):
    high = value.astype(BF16).astype(F32)
    rest = value - high
    middle = rest.astype(BF16).astype(F32)
    return high, middle, rest - middle


def pick_lanes(table, index):
    spread = jnp.broadcast_to(index, table.shape)
    return jnp.take_along_axis(table, spread, axis=1, mode="promise_in_bounds")


def prepare_kernel(points, surface, displacement, rotation, halo, message, lent):
    at = [surface[i : i + 1, :] for i in range(3)]
    turn = [rotation[i : i + 1, :] for i in range(3)]
    rotated = cross3(turn, at)
    term = [displacement[i : i + 1, :] - rotated[i] for i in range(3)]
    body = jnp.concatenate(term + turn[:2] + at, axis=0)
    last = jnp.concatenate([turn[2][:, i * LANES : (i + 1) * LANES] for i in range(SIDE)], axis=0)
    whole = jnp.concatenate([body, last], axis=1)
    for i in range(SIDE):
        message[i] = whole
    table = jnp.concatenate([points[...], jnp.zeros((5, LANES), F32)], axis=0)
    lent[...] = pick_lanes(table, halo[0:1, :])


def sums_kernel(place, nodes, surface, message, near, left, right, terms, total, sums, spots):
    row = rows_of((SIDE, LANES))
    lane = lanes_of((SIDE, LANES))
    outer = jnp.where(
        lane < 32,
        nodes[0],
        pltpu.roll(nodes[SIDE - 1], 32, axis=1),
    )
    outer = pltpu.roll(outer, 5, axis=0)
    for block in range(SIDE + 1):
        value = nodes[block] if block < SIDE else outer
        square = value[5:6] * value[5:6] + value[6:7] * value[6:7] + value[7:8] * value[7:8] + SOFTENING
        side = jnp.where(row >= 5, -2.0 * value, jnp.where(row == 3, 1.0, jnp.where(row == 4, square, 0.0)))
        high, middle, low = in_three(side)
        stack = [high, high, high, middle, middle, low, middle, low]
        stack = jnp.concatenate(stack + [jnp.zeros_like(high)] * 8, axis=0)
        left[block * LANES : (block + 1) * LANES, :] = stack.T.astype(BF16)[:, :64]
    width = surface.shape[2] - LANES
    line = rows_of((SIDE, width))
    for part in range(SIDE):
        value = surface[part][:, :width]
        tail = surface[part][:, width:]
        tail = jnp.concatenate([tail[i : i + 1] for i in range(SIDE)], axis=1)
        square = value[5:6] * value[5:6] + value[6:7] * value[6:7] + value[7:8] * value[7:8]
        side = jnp.where(line >= 5, value, jnp.where(line == 3, square, jnp.where(line == 4, 1.0, 0.0)))
        high, middle, low = in_three(side)
        stack = jnp.concatenate([high, middle, low, high, middle, high, low, middle], axis=0)
        right[:, part * width : (part + 1) * width] = stack.astype(BF16)
        term = jnp.where(line < 5, value, jnp.where(line == 5, tail, jnp.where(line == 6, 1.0, 0.0)))
        high, middle, _ = in_three(term)
        terms[:, part * width : (part + 1) * width] = jnp.concatenate([high, middle], axis=0).astype(BF16)
    total[...] = jnp.zeros_like(total)
    across = right.shape[1] // SURF_STEP

    def step(i, carry):
        n = pl.multiple_of((i // across) * NODE_STEP, LANES)
        s = pl.multiple_of((i % across) * SURF_STEP, LANES)
        spread = jnp.dot(left[pl.ds(n, NODE_STEP), :], right[:, pl.ds(s, SURF_STEP)], preferred_element_type=F32)
        inverse = lax.rsqrt(spread)
        weight = inverse * inverse * inverse
        high = weight.astype(BF16)
        low = (weight - high.astype(F32)).astype(BF16)
        term = terms[:, pl.ds(s, SURF_STEP)]
        total[pl.ds(n, NODE_STEP), :] += lax.dot_general(
            high, term, NT, preferred_element_type=F32
        ) + lax.dot_general(low, term, NT, preferred_element_type=F32)
        return carry

    lax.fori_loop(0, (SIDE + 1) * LANES // NODE_STEP * across, step, 0)

    for block in range(SIDE + 1):
        both = total[block * LANES : (block + 1) * LANES, :]
        both = jnp.concatenate([both, jnp.zeros((LANES, LANES - 16), F32)], axis=1).T
        value = both[:SIDE] + both[SIDE : 2 * SIDE]
        if block < SIDE:
            message[block, :, :LANES] = value
            index = nodes[block][3:4].astype(jnp.int32)
            sums[block + 1] = pick_lanes(value, index)
            spots[block + 1] = pick_lanes(nodes[block], index)
        else:
            sums[0] = value
            sums[SIDE + 1] = pltpu.roll(value, LANES - 32, axis=1)
            spots[0] = outer
            spots[SIDE + 1] = pltpu.roll(outer, LANES - 32, axis=1)
    for block in range(SIDE):
        message[block, :, LANES:] = jnp.where(lane < 32, sums[block], pltpu.roll(sums[block + 2], 32, axis=1))
    here = place[0]
    near[:, :LANES] = nodes[here]
    near[:, LANES:] = jnp.where(lane < 32, spots[here], pltpu.roll(spots[here + 2], 32, axis=1))


def swept_kernel(received, near, cells, motion_out, swept_out):
    total = received[0]
    for i in range(1, SIDE):
        total = total + received[i]
    top = [total[i : i + 1] for i in range(3)]
    turn = [total[i : i + 1] for i in range(3, 6)]
    spot = [near[i : i + 1, :] for i in range(5, 8)]
    turned = cross3(turn, spot)
    motion = [(top[i] + turned[i]) / total[6:7] for i in range(3)]
    motion_out[...] = jnp.concatenate([m[:, :LANES] for m in motion], axis=0)
    table = jnp.concatenate(spot + motion + [jnp.zeros_like(spot[0])] * 2, axis=0)
    own, lent = table[:, :LANES], table[:, LANES:]
    count = cells.shape[1]
    for group in range(count // LANES):
        corner = []
        for a in range(4):
            index = cells[a : a + 1, group * LANES : (group + 1) * LANES]
            inside = (index >= 32) & (index < 160)
            from_own = pick_lanes(own, jnp.where(inside, index - 32, 0))
            from_lent = pick_lanes(lent, jnp.where(inside, 0, jnp.where(index < 32, index, index - 128)))
            corner.append(jnp.where(jnp.broadcast_to(inside, own.shape), from_own, from_lent))
        move = [[c[3 + i : 4 + i] for i in range(3)] for c in corner]
        half = [[c[i : i + 1] + 0.5 * c[3 + i : 4 + i] for i in range(3)] for c in corner]
        result = jnp.zeros((1, LANES), F32)
        for p, q, r in ((1, 2, 3), (0, 3, 2), (0, 1, 3), (0, 2, 1)):
            one = [half[q][i] - half[p][i] for i in range(3)]
            two = [half[r][i] - half[p][i] for i in range(3)]
            normal = cross3(one, two)
            for i in range(3):
                average = (move[p][i] + move[q][i] + move[r][i]) / 3.0
                result = result + average * (0.5 * normal[i])
        swept_out[group : group + 1, :] = result


def shards(points, surface, displacement, rotation, halo_index, connectivity):
    width = surface.shape[1]
    nodes = points.shape[1]
    lend = halo_index.shape[0]
    halo = jnp.pad(halo_index[None, :], ((0, 7), (0, nodes - lend)))
    message, lent = pl.pallas_call(
        prepare_kernel,
        out_shape=(
            jax.ShapeDtypeStruct((SIDE, 8, width + LANES), F32),
            jax.ShapeDtypeStruct((8, LANES), F32),
        ),
    )(points, surface, displacement, rotation, halo)
    blocks = lax.axis_size("vol") * SIDE * SIDE
    ends = []
    for b in range(SIDE - 1, blocks, SIDE):
        ends += [(b, (b + 1) % blocks), ((b + 1) % blocks, b)]
    outer = lax.ppermute(lent[:3], ("vol", "z", "y"), ends)
    surfaces = lax.all_to_all(message, "z", 0, 0)
    own = jnp.concatenate(
        [outer, halo[:1].astype(F32), jnp.zeros((1, nodes), F32), points], axis=0
    )
    around = lax.all_to_all(jnp.broadcast_to(own[None], (SIDE, 8, nodes)), "y", 0, 0)
    place = lax.axis_index("y").astype(jnp.int32).reshape(1)
    vmem = pl.BlockSpec(memory_space=pltpu.VMEM)
    partial, near = pl.pallas_call(
        sums_kernel,
        out_shape=(
            jax.ShapeDtypeStruct((SIDE, 8, 2 * LANES), F32),
            jax.ShapeDtypeStruct((8, 2 * LANES), F32),
        ),
        in_specs=[pl.BlockSpec(memory_space=pltpu.SMEM), vmem, vmem],
        out_specs=(vmem, vmem),
        scratch_shapes=[
            pltpu.VMEM(((SIDE + 1) * LANES, 64), BF16),
            pltpu.VMEM((64, SIDE * width), BF16),
            pltpu.VMEM((16, SIDE * width), BF16),
            pltpu.VMEM(((SIDE + 1) * LANES, 16), F32),
            pltpu.VMEM((SIDE + 2, 8, LANES), F32),
            pltpu.VMEM((SIDE + 2, 8, LANES), F32),
        ],
        compiler_params=pltpu.CompilerParams(vmem_limit_bytes=40 << 20),
    )(place, around, surfaces)
    received = lax.all_to_all(partial, "y", 0, 0)
    count = connectivity.shape[1]
    motion, swept = pl.pallas_call(
        swept_kernel,
        out_shape=(
            jax.ShapeDtypeStruct((3, nodes), F32),
            jax.ShapeDtypeStruct((count // LANES, LANES), F32),
        ),
    )(received, near, connectivity)
    return motion, swept.reshape(count)


def solution(mesh):
    split = Mesh(mesh.devices.reshape(mesh.devices.shape[0], SIDE, SIDE), ("vol", "z", "y"))
    nodes = ("vol", "z", "y")
    surface = P(None, ("z", "y"))
    in_specs = (P(None, nodes), surface, surface, surface, P(nodes), P(None, nodes))
    out_specs = (P(None, nodes), P(nodes))
    return jax.shard_map(shards, mesh=split, in_specs=in_specs, out_specs=out_specs, check_vma=False)
```

```python
import jax
import jax.numpy as jnp
from jax import lax
from jax.experimental import pallas as pl
from jax.experimental.pallas import tpu as pltpu
from jax.sharding import Mesh
from jax.sharding import PartitionSpec as P

SOFTENING = 0.01
F32 = jnp.float32
BF16 = jnp.bfloat16
SIDE = 8
LANES = 128
OWN_STEP = 2048
SURF_STEP = 2048


def rows_of(shape):
    return lax.broadcasted_iota(jnp.int32, shape, 0)


def lanes_of(shape):
    return lax.broadcasted_iota(jnp.int32, shape, 1)


def cross3(a, b):
    return (
        a[1] * b[2] - a[2] * b[1],
        a[2] * b[0] - a[0] * b[2],
        a[0] * b[1] - a[1] * b[0],
    )


def in_three(value):
    high = value.astype(BF16).astype(F32)
    rest = value - high
    middle = rest.astype(BF16).astype(F32)
    return high, middle, rest - middle


def pick_lanes(table, index):
    spread = jnp.broadcast_to(index, table.shape)
    return jnp.take_along_axis(table, spread, axis=1, mode="promise_in_bounds")


def prepare_kernel(points, surface, displacement, rotation, halo, message, own, lent, index):
    at = [surface[i : i + 1, :] for i in range(3)]
    turn = [rotation[i : i + 1, :] for i in range(3)]
    rotated = cross3(turn, at)
    term = [displacement[i : i + 1, :] - rotated[i] for i in range(3)]
    body = jnp.concatenate(term + turn[:2] + at, axis=0)
    last = jnp.concatenate([turn[2][:, i * LANES : (i + 1) * LANES] for i in range(SIDE)], axis=0)
    whole = jnp.concatenate([body, last], axis=1)
    for i in range(SIDE):
        message[i] = whole
    index[...] = jnp.zeros_like(index)
    index[0:1, 0 : halo.shape[1]] = halo[...]
    place = index[0:1, :]
    own[...] = jnp.concatenate(
        [jnp.zeros((3, LANES), F32), place.astype(F32), jnp.zeros((1, LANES), F32), points[...]], axis=0
    )
    table = jnp.concatenate([points[...], jnp.zeros((5, LANES), F32)], axis=0)
    lent[...] = jnp.where(rows_of(table.shape) < 3, pick_lanes(table, place), 0.0)


def node_side(value):
    row = rows_of(value.shape)
    square = value[5:6] * value[5:6] + value[6:7] * value[6:7] + value[7:8] * value[7:8] + SOFTENING
    side = jnp.where(row >= 5, -2.0 * value, jnp.where(row == 3, 1.0, jnp.where(row == 4, square, 0.0)))
    high, middle, low = in_three(side)
    stack = [high, high, high, middle, middle, low, middle, low] + [jnp.zeros_like(high)] * 8
    return jnp.concatenate(stack, axis=0).astype(BF16)


def surface_side(value):
    row = rows_of(value.shape)
    square = value[5:6] * value[5:6] + value[6:7] * value[6:7] + value[7:8] * value[7:8]
    side = jnp.where(row >= 5, value, jnp.where(row == 3, square, jnp.where(row == 4, 1.0, 0.0)))
    high, middle, low = in_three(side)
    stack = [high, middle, low, high, middle, high, low, middle] + [jnp.zeros_like(high)] * 8
    return jnp.concatenate(stack, axis=0).T.astype(BF16)


def add_sums(right, terms, left, total, surf_step):
    def step(i, carry):
        s = pl.multiple_of(i * surf_step, LANES)
        spread = jnp.dot(right[pl.ds(s, surf_step), :], left[...], preferred_element_type=F32)
        inverse = lax.rsqrt(spread)
        weight = inverse * inverse * inverse
        high = weight.astype(BF16)
        low = (weight - high.astype(F32)).astype(BF16)
        term = terms[:, pl.ds(s, surf_step)]
        total[...] += jnp.dot(term, high, preferred_element_type=F32) + jnp.dot(
            term, low, preferred_element_type=F32
        )
        return carry

    total[...] = jnp.zeros_like(total)
    lax.fori_loop(0, right.shape[0] // surf_step, step, 0)


def own_kernel(own, surface, right, terms, sums, left, total):
    width = surface.shape[2] - LANES
    line = rows_of((SIDE, width))
    for part in range(SIDE):
        value = surface[part][:, :width]
        tail = surface[part][:, width:]
        tail = jnp.concatenate([tail[i : i + 1] for i in range(SIDE)], axis=1)
        right[part * width : (part + 1) * width, :] = surface_side(value)
        term = jnp.where(line < 5, value, jnp.where(line == 5, tail, jnp.where(line == 6, 1.0, 0.0)))
        high, middle, _ = in_three(term)
        terms[:, part * width : (part + 1) * width] = jnp.concatenate([high, middle], axis=0).astype(BF16)
    left[...] = node_side(own[...])
    add_sums(right, terms, left, total, OWN_STEP)
    sums[...] = total[:SIDE] + total[SIDE:]


def sums_kernel(place, nodes, right, terms, own_sums, message, near, left, total, sums, spots):
    lane = lanes_of((SIDE, LANES))
    here = place[0]
    outer = jnp.where(lane < 32, nodes[0], pltpu.roll(nodes[SIDE - 1], 32, axis=1))
    outer = pltpu.roll(outer, 5, axis=0)
    for k in range(SIDE):
        value = nodes[(here + k + 1) % SIDE] if k < SIDE - 1 else outer
        left[:, k * LANES : (k + 1) * LANES] = node_side(value)
    add_sums(right, terms, left, total, SURF_STEP)
    whole = total[:SIDE] + total[SIDE:]

    def keep(block, value):
        message[block, :, :LANES] = value
        index = nodes[block][3:4].astype(jnp.int32)
        sums[block + 1] = pick_lanes(value, index)
        spots[block + 1] = pick_lanes(nodes[block], index)

    keep(here, own_sums[...])
    for k in range(SIDE - 1):
        keep((here + k + 1) % SIDE, whole[:, k * LANES : (k + 1) * LANES])
    value = whole[:, (SIDE - 1) * LANES :]
    sums[0] = value
    sums[SIDE + 1] = pltpu.roll(value, LANES - 32, axis=1)
    spots[0] = outer
    spots[SIDE + 1] = pltpu.roll(outer, LANES - 32, axis=1)
    for block in range(SIDE):
        message[block, :, LANES:] = jnp.where(lane < 32, sums[block], pltpu.roll(sums[block + 2], 32, axis=1))
    near[:, :LANES] = nodes[here]
    near[:, LANES:] = jnp.where(lane < 32, spots[here], pltpu.roll(spots[here + 2], 32, axis=1))


def swept_kernel(received, near, cells, motion_out, swept_out):
    total = received[0]
    for i in range(1, SIDE):
        total = total + received[i]
    top = [total[i : i + 1] for i in range(3)]
    turn = [total[i : i + 1] for i in range(3, 6)]
    spot = [near[i : i + 1, :] for i in range(5, 8)]
    turned = cross3(turn, spot)
    motion = [(top[i] + turned[i]) / total[6:7] for i in range(3)]
    motion_out[...] = jnp.concatenate([m[:, :LANES] for m in motion], axis=0)
    table = jnp.concatenate(spot + motion + [jnp.zeros_like(spot[0])] * 2, axis=0)
    own, lent = table[:, :LANES], table[:, LANES:]
    count = cells.shape[1]
    for group in range(count // LANES):
        corner = []
        for a in range(4):
            index = cells[a : a + 1, group * LANES : (group + 1) * LANES]
            inside = (index >= 32) & (index < 160)
            from_own = pick_lanes(own, jnp.where(inside, index - 32, 0))
            from_lent = pick_lanes(lent, jnp.where(inside, 0, jnp.where(index < 32, index, index - 128)))
            corner.append(jnp.where(jnp.broadcast_to(inside, own.shape), from_own, from_lent))
        move = [[c[3 + i : 4 + i] for i in range(3)] for c in corner]
        half = [[c[i : i + 1] + 0.5 * c[3 + i : 4 + i] for i in range(3)] for c in corner]
        result = jnp.zeros((1, LANES), F32)
        for p, q, r in ((1, 2, 3), (0, 3, 2), (0, 1, 3), (0, 2, 1)):
            one = [half[q][i] - half[p][i] for i in range(3)]
            two = [half[r][i] - half[p][i] for i in range(3)]
            normal = cross3(one, two)
            for i in range(3):
                average = (move[p][i] + move[q][i] + move[r][i]) / 3.0
                result = result + average * (0.5 * normal[i])
        swept_out[group : group + 1, :] = result


def shards(points, surface, displacement, rotation, halo_index, connectivity):
    width = surface.shape[1]
    nodes = points.shape[1]
    lend = halo_index.shape[0]
    message, own, lent = pl.pallas_call(
        prepare_kernel,
        out_shape=(
            jax.ShapeDtypeStruct((SIDE, 8, width + LANES), F32),
            jax.ShapeDtypeStruct((8, LANES), F32),
            jax.ShapeDtypeStruct((8, LANES), F32),
        ),
        scratch_shapes=[pltpu.VMEM((8, LANES), jnp.int32)],
    )(points, surface, displacement, rotation, halo_index.reshape(1, lend))
    blocks = lax.axis_size("vol") * SIDE * SIDE
    ends = []
    for b in range(SIDE - 1, blocks, SIDE):
        ends += [(b, (b + 1) % blocks), ((b + 1) % blocks, b)]
    outer = lax.ppermute(lent, ("vol", "z", "y"), ends)
    surfaces = lax.all_to_all(message, "z", 0, 0)
    surfaces, own, outer = lax.optimization_barrier((surfaces, own, outer))
    repeated = jnp.broadcast_to((own + outer)[None], (SIDE, 8, nodes))
    around = lax.all_to_all(repeated, "y", 0, 0)
    total_surface = SIDE * width
    right, terms, own_sums = pl.pallas_call(
        own_kernel,
        out_shape=(
            jax.ShapeDtypeStruct((total_surface, LANES), BF16),
            jax.ShapeDtypeStruct((16, total_surface), BF16),
            jax.ShapeDtypeStruct((8, LANES), F32),
        ),
        scratch_shapes=[pltpu.VMEM((LANES, LANES), BF16), pltpu.VMEM((16, LANES), F32)],
        compiler_params=pltpu.CompilerParams(vmem_limit_bytes=24 << 20),
        cost_estimate=pl.CostEstimate(flops=5 * 10**9, bytes_accessed=3 << 20, transcendentals=1 << 20),
    )(own, surfaces)
    place = lax.axis_index("y").astype(jnp.int32).reshape(1)
    vmem = pl.BlockSpec(memory_space=pltpu.VMEM)
    partial, near = pl.pallas_call(
        sums_kernel,
        out_shape=(
            jax.ShapeDtypeStruct((SIDE, 8, 2 * LANES), F32),
            jax.ShapeDtypeStruct((8, 2 * LANES), F32),
        ),
        in_specs=[pl.BlockSpec(memory_space=pltpu.SMEM), vmem, vmem, vmem, vmem],
        out_specs=(vmem, vmem),
        scratch_shapes=[
            pltpu.VMEM((LANES, SIDE * LANES), BF16),
            pltpu.VMEM((16, SIDE * LANES), F32),
            pltpu.VMEM((SIDE + 2, 8, LANES), F32),
            pltpu.VMEM((SIDE + 2, 8, LANES), F32),
        ],
        compiler_params=pltpu.CompilerParams(vmem_limit_bytes=40 << 20),
        cost_estimate=pl.CostEstimate(flops=30 * 10**9, bytes_accessed=3 << 20, transcendentals=8 << 20),
    )(place, around, right, terms, own_sums)
    received = lax.all_to_all(partial, "y", 0, 0)
    count = connectivity.shape[1]
    motion, swept = pl.pallas_call(
        swept_kernel,
        out_shape=(
            jax.ShapeDtypeStruct((3, nodes), F32),
            jax.ShapeDtypeStruct((count // LANES, LANES), F32),
        ),
    )(received, near, connectivity)
    return motion, swept.reshape(count)


def solution(mesh):
    split = Mesh(mesh.devices.reshape(mesh.devices.shape[0], SIDE, SIDE), ("vol", "z", "y"))
    nodes = ("vol", "z", "y")
    surface = P(None, ("z", "y"))
    in_specs = (P(None, nodes), surface, surface, surface, P(nodes), P(None, nodes))
    out_specs = (P(None, nodes), P(nodes))
    return jax.shard_map(shards, mesh=split, in_specs=in_specs, out_specs=out_specs, check_vma=False)
```

```python
import jax
import jax.numpy as jnp
from jax import lax
from jax.experimental import pallas as pl
from jax.experimental.pallas import tpu as pltpu
from jax.sharding import Mesh
from jax.sharding import PartitionSpec as P

SOFTENING = 0.01
F32 = jnp.float32
BF16 = jnp.bfloat16
SIDE = 8
LANES = 128
OWN_STEP = 2048
SURF_STEP = 4096


def rows_of(shape):
    return lax.broadcasted_iota(jnp.int32, shape, 0)


def lanes_of(shape):
    return lax.broadcasted_iota(jnp.int32, shape, 1)


def cross3(a, b):
    return (
        a[1] * b[2] - a[2] * b[1],
        a[2] * b[0] - a[0] * b[2],
        a[0] * b[1] - a[1] * b[0],
    )


def in_three(value):
    high = value.astype(BF16).astype(F32)
    rest = value - high
    middle = rest.astype(BF16).astype(F32)
    return high, middle, rest - middle


def pick_lanes(table, index):
    spread = jnp.broadcast_to(index, table.shape)
    return jnp.take_along_axis(table, spread, axis=1, mode="promise_in_bounds")


def prepare_kernel(points, surface, displacement, rotation, halo, message, own, lent, index):
    at = [surface[i : i + 1, :] for i in range(3)]
    turn = [rotation[i : i + 1, :] for i in range(3)]
    rotated = cross3(turn, at)
    term = [displacement[i : i + 1, :] - rotated[i] for i in range(3)]
    body = jnp.concatenate(term + turn[:2] + at, axis=0)
    last = jnp.concatenate([turn[2][:, i * LANES : (i + 1) * LANES] for i in range(SIDE)], axis=0)
    whole = jnp.concatenate([body, last], axis=1)
    for i in range(SIDE):
        message[i] = whole
    index[...] = jnp.zeros_like(index)
    index[0:1, 0 : halo.shape[1]] = halo[...]
    place = index[0:1, :]
    mine = jnp.concatenate(
        [jnp.zeros((3, LANES), F32), place.astype(F32), jnp.zeros((1, LANES), F32), points[...]], axis=0
    )
    for i in range(SIDE):
        own[i] = mine
    table = jnp.concatenate([points[...], jnp.zeros((5, LANES), F32)], axis=0)
    lent[...] = jnp.where(rows_of(table.shape) < 3, pick_lanes(table, place), 0.0)


def node_side(value):
    row = rows_of(value.shape)
    square = value[5:6] * value[5:6] + value[6:7] * value[6:7] + value[7:8] * value[7:8] + SOFTENING
    side = jnp.where(row >= 5, -2.0 * value, jnp.where(row == 3, 1.0, jnp.where(row == 4, square, 0.0)))
    high, middle, low = in_three(side)
    stack = [high, high, high, middle, middle, low, middle, low] + [jnp.zeros_like(high)] * 8
    return jnp.concatenate(stack, axis=0).astype(BF16)


def surface_side(value):
    row = rows_of(value.shape)
    square = value[5:6] * value[5:6] + value[6:7] * value[6:7] + value[7:8] * value[7:8]
    side = jnp.where(row >= 5, value, jnp.where(row == 3, square, jnp.where(row == 4, 1.0, 0.0)))
    high, middle, low = in_three(side)
    stack = [high, middle, low, high, middle, high, low, middle] + [jnp.zeros_like(high)] * 8
    return jnp.concatenate(stack, axis=0).T.astype(BF16)


def add_sums(right, terms, left, total, surf_step):
    def step(i, carry):
        s = pl.multiple_of(i * surf_step, LANES)
        spread = jnp.dot(right[pl.ds(s, surf_step), :], left[...], preferred_element_type=F32)
        inverse = lax.rsqrt(spread)
        weight = inverse * inverse * inverse
        high = weight.astype(BF16)
        low = (weight - high.astype(F32)).astype(BF16)
        term = terms[:, pl.ds(s, surf_step)]
        total[...] += jnp.dot(term, high, preferred_element_type=F32) + jnp.dot(
            term, low, preferred_element_type=F32
        )
        return carry

    total[...] = jnp.zeros_like(total)
    lax.fori_loop(0, right.shape[0] // surf_step, step, 0)


def own_kernel(points, surface, right, terms, sums, left, total):
    width = surface.shape[2] - LANES
    line = rows_of((SIDE, width))
    for part in range(SIDE):
        value = surface[part][:, :width]
        tail = surface[part][:, width:]
        tail = jnp.concatenate([tail[i : i + 1] for i in range(SIDE)], axis=1)
        right[part * width : (part + 1) * width, :] = surface_side(value)
        term = jnp.where(line < 5, value, jnp.where(line == 5, tail, jnp.where(line == 6, 1.0, 0.0)))
        high, middle, _ = in_three(term)
        terms[:, part * width : (part + 1) * width] = jnp.concatenate([high, middle], axis=0).astype(BF16)
    left[...] = node_side(jnp.concatenate([jnp.zeros((5, LANES), F32), points[...]], axis=0))
    add_sums(right, terms, left, total, OWN_STEP)
    sums[...] = total[:SIDE] + total[SIDE:]


def sums_kernel(place, nodes, right, terms, own_sums, message, near, left, total, sums, spots):
    lane = lanes_of((SIDE, LANES))
    here = place[0]
    outer = jnp.where(lane < 32, nodes[SIDE - 1], pltpu.roll(nodes[0], 32, axis=1))
    outer = pltpu.roll(outer, 5, axis=0)
    for k in range(SIDE):
        value = nodes[(here + k + 1) % SIDE] if k < SIDE - 1 else outer
        left[:, k * LANES : (k + 1) * LANES] = node_side(value)
    add_sums(right, terms, left, total, SURF_STEP)
    whole = total[:SIDE] + total[SIDE:]

    def keep(block, value):
        message[block, :, :LANES] = value
        index = nodes[block][3:4].astype(jnp.int32)
        sums[block + 1] = pick_lanes(value, index)
        spots[block + 1] = pick_lanes(nodes[block], index)

    keep(here, own_sums[...])
    for k in range(SIDE - 1):
        keep((here + k + 1) % SIDE, whole[:, k * LANES : (k + 1) * LANES])
    value = whole[:, (SIDE - 1) * LANES :]
    sums[0] = value
    sums[SIDE + 1] = pltpu.roll(value, LANES - 32, axis=1)
    spots[0] = outer
    spots[SIDE + 1] = pltpu.roll(outer, LANES - 32, axis=1)
    for block in range(SIDE):
        message[block, :, LANES:] = jnp.where(lane < 32, sums[block], pltpu.roll(sums[block + 2], 32, axis=1))
    near[:, :LANES] = nodes[here]
    near[:, LANES:] = jnp.where(lane < 32, spots[here], pltpu.roll(spots[here + 2], 32, axis=1))


def swept_kernel(received, near, cells, motion_out, swept_out):
    total = received[0]
    for i in range(1, SIDE):
        total = total + received[i]
    top = [total[i : i + 1] for i in range(3)]
    turn = [total[i : i + 1] for i in range(3, 6)]
    spot = [near[i : i + 1, :] for i in range(5, 8)]
    turned = cross3(turn, spot)
    motion = [(top[i] + turned[i]) / total[6:7] for i in range(3)]
    motion_out[...] = jnp.concatenate([m[:, :LANES] for m in motion], axis=0)
    table = jnp.concatenate(spot + motion + [jnp.zeros_like(spot[0])] * 2, axis=0)
    own, lent = table[:, :LANES], table[:, LANES:]
    count = cells.shape[1]
    for group in range(count // LANES):
        corner = []
        for a in range(4):
            index = cells[a : a + 1, group * LANES : (group + 1) * LANES]
            inside = (index >= 32) & (index < 160)
            from_own = pick_lanes(own, jnp.where(inside, index - 32, 0))
            from_lent = pick_lanes(lent, jnp.where(inside, 0, jnp.where(index < 32, index, index - 128)))
            corner.append(jnp.where(jnp.broadcast_to(inside, own.shape), from_own, from_lent))
        move = [[c[3 + i : 4 + i] for i in range(3)] for c in corner]
        half = [[c[i : i + 1] + 0.5 * c[3 + i : 4 + i] for i in range(3)] for c in corner]
        result = jnp.zeros((1, LANES), F32)
        for p, q, r in ((1, 2, 3), (0, 3, 2), (0, 1, 3), (0, 2, 1)):
            one = [half[q][i] - half[p][i] for i in range(3)]
            two = [half[r][i] - half[p][i] for i in range(3)]
            normal = cross3(one, two)
            for i in range(3):
                average = (move[p][i] + move[q][i] + move[r][i]) / 3.0
                result = result + average * (0.5 * normal[i])
        swept_out[group : group + 1, :] = result


def shards(points, surface, displacement, rotation, halo_index, connectivity):
    width = surface.shape[1]
    nodes = points.shape[1]
    lend = halo_index.shape[0]
    message, own, lent = pl.pallas_call(
        prepare_kernel,
        out_shape=(
            jax.ShapeDtypeStruct((SIDE, 8, width + LANES), F32),
            jax.ShapeDtypeStruct((SIDE, 8, LANES), F32),
            jax.ShapeDtypeStruct((8, LANES), F32),
        ),
        scratch_shapes=[pltpu.VMEM((8, LANES), jnp.int32)],
    )(points, surface, displacement, rotation, halo_index.reshape(1, lend))
    rows = lax.axis_size("vol") * SIDE
    ends = []
    for row in range(rows):
        after = (row + 1) % rows
        ends += [(row * SIDE + SIDE - 1, after * SIDE + SIDE - 1), (after * SIDE, row * SIDE)]
    outer = lax.ppermute(lent, ("vol", "z", "y"), ends)
    surfaces = lax.all_to_all(message, "z", 0, 0)
    surfaces, own, outer = lax.optimization_barrier((surfaces, own, outer))
    around = lax.all_to_all(own + outer, "y", 0, 0)
    total_surface = SIDE * width
    right, terms, own_sums = pl.pallas_call(
        own_kernel,
        out_shape=(
            jax.ShapeDtypeStruct((total_surface, LANES), BF16),
            jax.ShapeDtypeStruct((16, total_surface), BF16),
            jax.ShapeDtypeStruct((8, LANES), F32),
        ),
        scratch_shapes=[pltpu.VMEM((LANES, LANES), BF16), pltpu.VMEM((16, LANES), F32)],
        compiler_params=pltpu.CompilerParams(vmem_limit_bytes=24 << 20),
        cost_estimate=pl.CostEstimate(flops=5 * 10**9, bytes_accessed=3 << 20, transcendentals=1 << 20),
    )(points, surfaces)
    place = lax.axis_index("y").astype(jnp.int32).reshape(1)
    vmem = pl.BlockSpec(memory_space=pltpu.VMEM)
    partial, near = pl.pallas_call(
        sums_kernel,
        out_shape=(
            jax.ShapeDtypeStruct((SIDE, 8, 2 * LANES), F32),
            jax.ShapeDtypeStruct((8, 2 * LANES), F32),
        ),
        in_specs=[pl.BlockSpec(memory_space=pltpu.SMEM), vmem, vmem, vmem, vmem],
        out_specs=(vmem, vmem),
        scratch_shapes=[
            pltpu.VMEM((LANES, SIDE * LANES), BF16),
            pltpu.VMEM((16, SIDE * LANES), F32),
            pltpu.VMEM((SIDE + 2, 8, LANES), F32),
            pltpu.VMEM((SIDE + 2, 8, LANES), F32),
        ],
        compiler_params=pltpu.CompilerParams(vmem_limit_bytes=40 << 20),
        cost_estimate=pl.CostEstimate(flops=30 * 10**9, bytes_accessed=3 << 20, transcendentals=8 << 20),
    )(place, around, right, terms, own_sums)
    received = lax.all_to_all(partial, "y", 0, 0)
    count = connectivity.shape[1]
    motion, swept = pl.pallas_call(
        swept_kernel,
        out_shape=(
            jax.ShapeDtypeStruct((3, nodes), F32),
            jax.ShapeDtypeStruct((count // LANES, LANES), F32),
        ),
        compiler_params=pltpu.CompilerParams(vmem_limit_bytes=8 << 20),
    )(received, near, connectivity)
    return motion, swept.reshape(count)


def solution(mesh):
    split = Mesh(mesh.devices.reshape(mesh.devices.shape[0], SIDE, SIDE), ("vol", "z", "y"))
    nodes = ("vol", "z", "y")
    surface = P(None, ("z", "y"))
    in_specs = (P(None, nodes), surface, surface, surface, P(nodes), P(None, nodes))
    out_specs = (P(None, nodes), P(nodes))
    return jax.shard_map(shards, mesh=split, in_specs=in_specs, out_specs=out_specs, check_vma=False)
```

```python
import jax
import jax.numpy as jnp
from jax import lax
from jax.experimental import pallas as pl
from jax.experimental.pallas import tpu as pltpu
from jax.sharding import Mesh
from jax.sharding import PartitionSpec as P

SOFTENING = 0.01
F32 = jnp.float32
BF16 = jnp.bfloat16
SIDE = 8
LANES = 128
OWN_STEP = 8192
SURF_STEP = 4096


def rows_of(shape):
    return lax.broadcasted_iota(jnp.int32, shape, 0)


def lanes_of(shape):
    return lax.broadcasted_iota(jnp.int32, shape, 1)


def cross3(a, b):
    return (
        a[1] * b[2] - a[2] * b[1],
        a[2] * b[0] - a[0] * b[2],
        a[0] * b[1] - a[1] * b[0],
    )


def in_three(value):
    high = value.astype(BF16).astype(F32)
    rest = value - high
    middle = rest.astype(BF16).astype(F32)
    return high, middle, rest - middle


def pick_lanes(table, index):
    spread = jnp.broadcast_to(index, table.shape)
    return jnp.take_along_axis(table, spread, axis=1, mode="promise_in_bounds")


def prepare_kernel(points, surface, displacement, rotation, halo, message, own, lent, index):
    at = [surface[i : i + 1, :] for i in range(3)]
    turn = [rotation[i : i + 1, :] for i in range(3)]
    rotated = cross3(turn, at)
    term = [displacement[i : i + 1, :] - rotated[i] for i in range(3)]
    body = jnp.concatenate(term + turn[:2] + at, axis=0)
    last = jnp.concatenate([turn[2][:, i * LANES : (i + 1) * LANES] for i in range(SIDE)], axis=0)
    whole = jnp.concatenate([body, last], axis=1)
    for i in range(SIDE):
        message[i] = whole
    index[...] = jnp.zeros_like(index)
    index[0:1, 0 : halo.shape[1]] = halo[...]
    place = index[0:1, :]
    mine = jnp.concatenate(
        [jnp.zeros((3, LANES), F32), place.astype(F32), jnp.zeros((1, LANES), F32), points[...]], axis=0
    )
    for i in range(SIDE):
        own[i] = mine
    table = jnp.concatenate([points[...], jnp.zeros((5, LANES), F32)], axis=0)
    lent[...] = jnp.where(rows_of(table.shape) < 3, pick_lanes(table, place), 0.0)


def node_side(value):
    row = rows_of(value.shape)
    square = value[5:6] * value[5:6] + value[6:7] * value[6:7] + value[7:8] * value[7:8] + SOFTENING
    side = jnp.where(row >= 5, -2.0 * value, jnp.where(row == 3, 1.0, jnp.where(row == 4, square, 0.0)))
    high, middle, low = in_three(side)
    stack = [high, high, high, middle, middle, low, middle, low] + [jnp.zeros_like(high)] * 8
    return jnp.concatenate(stack, axis=0).astype(BF16)


def surface_side(value):
    row = rows_of(value.shape)
    square = value[5:6] * value[5:6] + value[6:7] * value[6:7] + value[7:8] * value[7:8]
    side = jnp.where(row >= 5, value, jnp.where(row == 3, square, jnp.where(row == 4, 1.0, 0.0)))
    high, middle, low = in_three(side)
    stack = [high, middle, low, high, middle, high, low, middle] + [jnp.zeros_like(high)] * 8
    return jnp.concatenate(stack, axis=0).T.astype(BF16)


def add_sums(right, terms, left, total, surf_step):
    def step(i, carry):
        s = pl.multiple_of(i * surf_step, LANES)
        spread = jnp.dot(right[pl.ds(s, surf_step), :], left[...], preferred_element_type=F32)
        inverse = lax.rsqrt(spread)
        weight = inverse * inverse * inverse
        high = weight.astype(BF16)
        low = (weight - high.astype(F32)).astype(BF16)
        term = terms[:, pl.ds(s, surf_step)]
        total[...] += jnp.dot(term, high, preferred_element_type=F32) + jnp.dot(
            term, low, preferred_element_type=F32
        )
        return carry

    total[...] = jnp.zeros_like(total)
    lax.fori_loop(0, right.shape[0] // surf_step, step, 0)


def own_kernel(points, surface, right, terms, sums, left, total):
    width = surface.shape[2] - LANES
    line = rows_of((SIDE, width))
    for part in range(SIDE):
        value = surface[part][:, :width]
        tail = surface[part][:, width:]
        tail = jnp.concatenate([tail[i : i + 1] for i in range(SIDE)], axis=1)
        right[part * width : (part + 1) * width, :] = surface_side(value)
        term = jnp.where(line < 5, value, jnp.where(line == 5, tail, jnp.where(line == 6, 1.0, 0.0)))
        high, middle, _ = in_three(term)
        terms[:, part * width : (part + 1) * width] = jnp.concatenate([high, middle], axis=0).astype(BF16)
    left[...] = node_side(jnp.concatenate([jnp.zeros((5, LANES), F32), points[...]], axis=0))
    add_sums(right, terms, left, total, OWN_STEP)
    sums[...] = total[:SIDE] + total[SIDE:]


def sums_kernel(place, nodes, right, terms, own_sums, message, near, left, total, sums, spots):
    lane = lanes_of((SIDE, LANES))
    here = place[0]
    outer = jnp.where(lane < 32, nodes[SIDE - 1], pltpu.roll(nodes[0], 32, axis=1))
    outer = pltpu.roll(outer, 5, axis=0)
    for k in range(SIDE):
        value = nodes[(here + k + 1) % SIDE] if k < SIDE - 1 else outer
        left[:, k * LANES : (k + 1) * LANES] = node_side(value)
    add_sums(right, terms, left, total, SURF_STEP)
    whole = total[:SIDE] + total[SIDE:]

    def keep(block, value):
        message[block, :, :LANES] = value
        index = nodes[block][3:4].astype(jnp.int32)
        sums[block + 1] = pick_lanes(value, index)
        spots[block + 1] = pick_lanes(nodes[block], index)

    keep(here, own_sums[...])
    for k in range(SIDE - 1):
        keep((here + k + 1) % SIDE, whole[:, k * LANES : (k + 1) * LANES])
    value = whole[:, (SIDE - 1) * LANES :]
    sums[0] = value
    sums[SIDE + 1] = pltpu.roll(value, LANES - 32, axis=1)
    spots[0] = outer
    spots[SIDE + 1] = pltpu.roll(outer, LANES - 32, axis=1)
    for block in range(SIDE):
        message[block, :, LANES:] = jnp.where(lane < 32, sums[block], pltpu.roll(sums[block + 2], 32, axis=1))
    near[:, :LANES] = nodes[here]
    near[:, LANES:] = jnp.where(lane < 32, spots[here], pltpu.roll(spots[here + 2], 32, axis=1))


def swept_kernel(received, near, cells, motion_out, swept_out):
    total = received[0]
    for i in range(1, SIDE):
        total = total + received[i]
    top = [total[i : i + 1] for i in range(3)]
    turn = [total[i : i + 1] for i in range(3, 6)]
    spot = [near[i : i + 1, :] for i in range(5, 8)]
    turned = cross3(turn, spot)
    motion = [(top[i] + turned[i]) / total[6:7] for i in range(3)]
    motion_out[...] = jnp.concatenate([m[:, :LANES] for m in motion], axis=0)
    table = jnp.concatenate(spot + motion + [jnp.zeros_like(spot[0])] * 2, axis=0)
    own, lent = table[:, :LANES], table[:, LANES:]
    count = cells.shape[1]
    for group in range(count // LANES):
        corner = []
        for a in range(4):
            index = cells[a : a + 1, group * LANES : (group + 1) * LANES]
            inside = (index >= 32) & (index < 160)
            from_own = pick_lanes(own, jnp.where(inside, index - 32, 0))
            from_lent = pick_lanes(lent, jnp.where(inside, 0, jnp.where(index < 32, index, index - 128)))
            corner.append(jnp.where(jnp.broadcast_to(inside, own.shape), from_own, from_lent))
        move = [[c[3 + i : 4 + i] for i in range(3)] for c in corner]
        half = [[c[i : i + 1] + 0.5 * c[3 + i : 4 + i] for i in range(3)] for c in corner]
        result = jnp.zeros((1, LANES), F32)
        for p, q, r in ((1, 2, 3), (0, 3, 2), (0, 1, 3), (0, 2, 1)):
            one = [half[q][i] - half[p][i] for i in range(3)]
            two = [half[r][i] - half[p][i] for i in range(3)]
            normal = cross3(one, two)
            for i in range(3):
                average = (move[p][i] + move[q][i] + move[r][i]) / 3.0
                result = result + average * (0.5 * normal[i])
        swept_out[group : group + 1, :] = result


def shards(points, surface, displacement, rotation, halo_index, connectivity):
    width = surface.shape[1]
    nodes = points.shape[1]
    lend = halo_index.shape[0]
    message, own, lent = pl.pallas_call(
        prepare_kernel,
        out_shape=(
            jax.ShapeDtypeStruct((SIDE, 8, width + LANES), F32),
            jax.ShapeDtypeStruct((SIDE, 8, LANES), F32),
            jax.ShapeDtypeStruct((8, LANES), F32),
        ),
        scratch_shapes=[pltpu.VMEM((8, LANES), jnp.int32)],
    )(points, surface, displacement, rotation, halo_index.reshape(1, lend))
    rows = lax.axis_size("vol") * SIDE
    ends = []
    for row in range(rows):
        after = (row + 1) % rows
        ends += [(row * SIDE + SIDE - 1, after * SIDE + SIDE - 1), (after * SIDE, row * SIDE)]
    outer = lax.ppermute(lent, ("vol", "z", "y"), ends)
    surfaces = lax.all_to_all(message, "z", 0, 0)
    surfaces, ready = lax.optimization_barrier((surfaces, own + outer))
    around = lax.all_to_all(ready, "y", 0, 0)
    total_surface = SIDE * width
    right, terms, own_sums = pl.pallas_call(
        own_kernel,
        out_shape=(
            jax.ShapeDtypeStruct((total_surface, LANES), BF16),
            jax.ShapeDtypeStruct((16, total_surface), BF16),
            jax.ShapeDtypeStruct((8, LANES), F32),
        ),
        scratch_shapes=[pltpu.VMEM((LANES, LANES), BF16), pltpu.VMEM((16, LANES), F32)],
        compiler_params=pltpu.CompilerParams(vmem_limit_bytes=24 << 20),
        cost_estimate=pl.CostEstimate(flops=5 * 10**9, bytes_accessed=3 << 20, transcendentals=1 << 20),
    )(points, surfaces)
    place = lax.axis_index("y").astype(jnp.int32).reshape(1)
    vmem = pl.BlockSpec(memory_space=pltpu.VMEM)
    partial, near = pl.pallas_call(
        sums_kernel,
        out_shape=(
            jax.ShapeDtypeStruct((SIDE, 8, 2 * LANES), F32),
            jax.ShapeDtypeStruct((8, 2 * LANES), F32),
        ),
        in_specs=[pl.BlockSpec(memory_space=pltpu.SMEM), vmem, vmem, vmem, vmem],
        out_specs=(vmem, vmem),
        scratch_shapes=[
            pltpu.VMEM((LANES, SIDE * LANES), BF16),
            pltpu.VMEM((16, SIDE * LANES), F32),
            pltpu.VMEM((SIDE + 2, 8, LANES), F32),
            pltpu.VMEM((SIDE + 2, 8, LANES), F32),
        ],
        compiler_params=pltpu.CompilerParams(vmem_limit_bytes=40 << 20),
        cost_estimate=pl.CostEstimate(flops=30 * 10**9, bytes_accessed=3 << 20, transcendentals=8 << 20),
    )(place, around, right, terms, own_sums)
    received = lax.all_to_all(partial, "y", 0, 0)
    count = connectivity.shape[1]
    motion, swept = pl.pallas_call(
        swept_kernel,
        out_shape=(
            jax.ShapeDtypeStruct((3, nodes), F32),
            jax.ShapeDtypeStruct((count // LANES, LANES), F32),
        ),
        compiler_params=pltpu.CompilerParams(vmem_limit_bytes=8 << 20),
    )(received, near, connectivity)
    return motion, swept.reshape(count)


def solution(mesh):
    split = Mesh(mesh.devices.reshape(mesh.devices.shape[0], SIDE, SIDE), ("vol", "z", "y"))
    nodes = ("vol", "z", "y")
    surface = P(None, ("z", "y"))
    in_specs = (P(None, nodes), surface, surface, surface, P(nodes), P(None, nodes))
    out_specs = (P(None, nodes), P(nodes))
    return jax.shard_map(shards, mesh=split, in_specs=in_specs, out_specs=out_specs, check_vma=False)
```

```python
import jax
import jax.numpy as jnp
from jax import lax
from jax.experimental import pallas as pl
from jax.experimental.pallas import tpu as pltpu
from jax.sharding import Mesh
from jax.sharding import PartitionSpec as P

SOFTENING = 0.01
F32 = jnp.float32
BF16 = jnp.bfloat16
SIDE = 8
LANES = 128
OWN_STEP = 8192
SURF_STEP = 4096


def rows_of(shape):
    return lax.broadcasted_iota(jnp.int32, shape, 0)


def lanes_of(shape):
    return lax.broadcasted_iota(jnp.int32, shape, 1)


def cross3(a, b):
    return (
        a[1] * b[2] - a[2] * b[1],
        a[2] * b[0] - a[0] * b[2],
        a[0] * b[1] - a[1] * b[0],
    )


def in_three(value):
    high = value.astype(BF16).astype(F32)
    rest = value - high
    middle = rest.astype(BF16).astype(F32)
    return high, middle, rest - middle


def pick_lanes(table, index):
    spread = jnp.broadcast_to(index, table.shape)
    return jnp.take_along_axis(table, spread, axis=1, mode="promise_in_bounds")


def prepare_kernel(points, surface, displacement, rotation, halo, message, own, lent, index):
    at = [surface[i : i + 1, :] for i in range(3)]
    turn = [rotation[i : i + 1, :] for i in range(3)]
    rotated = cross3(turn, at)
    term = [displacement[i : i + 1, :] - rotated[i] for i in range(3)]
    body = jnp.concatenate(term + turn[:2] + at, axis=0)
    last = jnp.concatenate([turn[2][:, i * LANES : (i + 1) * LANES] for i in range(SIDE)], axis=0)
    whole = jnp.concatenate([body, last], axis=1)
    for i in range(SIDE):
        message[i] = whole
    index[...] = jnp.zeros_like(index)
    index[0:1, 0 : halo.shape[1]] = halo[...]
    place = index[0:1, :]
    mine = jnp.concatenate(
        [jnp.zeros((3, LANES), F32), place.astype(F32), jnp.zeros((1, LANES), F32), points[...]], axis=0
    )
    for i in range(SIDE):
        own[i] = mine
    table = jnp.concatenate([points[...], jnp.zeros((5, LANES), F32)], axis=0)
    lent[...] = jnp.where(rows_of(table.shape) < 3, pick_lanes(table, place), 0.0)


def node_side(value):
    row = rows_of(value.shape)
    square = value[5:6] * value[5:6] + value[6:7] * value[6:7] + value[7:8] * value[7:8] + SOFTENING
    side = jnp.where(row >= 5, -2.0 * value, jnp.where(row == 3, 1.0, jnp.where(row == 4, square, 0.0)))
    high, middle, low = in_three(side)
    stack = [high, high, high, middle, middle, low, middle, low] + [jnp.zeros_like(high)] * 8
    return jnp.concatenate(stack, axis=0).astype(BF16)


def surface_side(value):
    row = rows_of(value.shape)
    square = value[5:6] * value[5:6] + value[6:7] * value[6:7] + value[7:8] * value[7:8]
    side = jnp.where(row >= 5, value, jnp.where(row == 3, square, jnp.where(row == 4, 1.0, 0.0)))
    high, middle, low = in_three(side)
    stack = [high, middle, low, high, middle, high, low, middle] + [jnp.zeros_like(high)] * 8
    return jnp.concatenate(stack, axis=0).T.astype(BF16)


def add_sums(right, terms, left, total, surf_step, first=0):
    def step(i, carry):
        s = pl.multiple_of(i * surf_step, LANES)
        spread = jnp.dot(right[pl.ds(s, surf_step), :], left[...], preferred_element_type=F32)
        inverse = lax.rsqrt(spread)
        weight = inverse * inverse * inverse
        high = weight.astype(BF16)
        low = (weight - high.astype(F32)).astype(BF16)
        term = terms[:, pl.ds(s, surf_step)]
        total[...] += jnp.dot(term, high, preferred_element_type=F32) + jnp.dot(
            term, low, preferred_element_type=F32
        )
        return carry

    lax.fori_loop(first // surf_step, right.shape[0] // surf_step, step, 0)


def surface_operands(surface, right, terms):
    width = surface.shape[2] - LANES
    line = rows_of((SIDE, width))
    for part in range(surface.shape[0]):
        value = surface[part][:, :width]
        tail = surface[part][:, width:]
        tail = jnp.concatenate([tail[i : i + 1] for i in range(SIDE)], axis=1)
        right[part * width : (part + 1) * width, :] = surface_side(value)
        term = jnp.where(line < 5, value, jnp.where(line == 5, tail, jnp.where(line == 6, 1.0, 0.0)))
        high, middle, _ = in_three(term)
        terms[:, part * width : (part + 1) * width] = jnp.concatenate([high, middle], axis=0).astype(BF16)


def early_kernel(nodes, surface, result, right, terms, left, total):
    surface_operands(surface, right, terms)
    for block in range(SIDE):
        left[:, block * LANES : (block + 1) * LANES] = node_side(nodes[block])
    total[...] = jnp.zeros_like(total)
    add_sums(right, terms, left, total, SURF_STEP)
    for block in range(SIDE):
        result[block, :SIDE] = nodes[block]
        result[block, SIDE:] = total[:, block * LANES : (block + 1) * LANES]


def own_kernel(flag, points, surface, before, right, terms, sums, left, total):
    surface_operands(surface, right, terms)

    @pl.when(flag[0] == 1)
    def _():
        for block in range(SIDE):
            left[:, block * LANES : (block + 1) * LANES] = node_side(before[block, :SIDE])
            total[:, block * LANES : (block + 1) * LANES] = before[block, SIDE:]
        add_sums(right, terms, left, total, SURF_STEP, right.shape[0] // 2)
        sums[...] = total[:SIDE] + total[SIDE:]

    @pl.when(flag[0] == 0)
    def _():
        left[:, :LANES] = node_side(jnp.concatenate([jnp.zeros((5, LANES), F32), points[...]], axis=0))
        total[:, :LANES] = jnp.zeros((16, LANES), F32)
        add_sums(right, terms, left.at[:, :LANES], total.at[:, :LANES], OWN_STEP)
        sums[:, :LANES] = total[:SIDE, :LANES] + total[SIDE:, :LANES]


def sums_kernel(place, nodes, right, terms, known, message, near, left, total, sums, spots):
    lane = lanes_of((SIDE, LANES))
    here, early = place[0], place[1]
    outer = jnp.where(lane < 32, nodes[SIDE - 1], pltpu.roll(nodes[0], 32, axis=1))
    outer = pltpu.roll(outer, 5, axis=0)
    end = (SIDE - 1) * LANES
    left[:, end:] = node_side(outer)
    total[...] = jnp.zeros_like(total)

    def keep(block, value):
        message[block, :, :LANES] = value
        index = nodes[block][3:4].astype(jnp.int32)
        sums[block + 1] = pick_lanes(value, index)
        spots[block + 1] = pick_lanes(nodes[block], index)

    @pl.when(early == 1)
    def _():
        add_sums(right, terms, left.at[:, end:], total.at[:, end:], OWN_STEP)
        for block in range(SIDE):
            keep(block, known[:, block * LANES : (block + 1) * LANES])

    @pl.when(early == 0)
    def _():
        for k in range(SIDE - 1):
            left[:, k * LANES : (k + 1) * LANES] = node_side(nodes[(here + k + 1) % SIDE])
        add_sums(right, terms, left, total, SURF_STEP)
        keep(here, known[:, :LANES])
        for k in range(SIDE - 1):
            part = total[:, k * LANES : (k + 1) * LANES]
            keep((here + k + 1) % SIDE, part[:SIDE] + part[SIDE:])

    value = total[:SIDE, end:] + total[SIDE:, end:]
    sums[0] = value
    sums[SIDE + 1] = pltpu.roll(value, LANES - 32, axis=1)
    spots[0] = outer
    spots[SIDE + 1] = pltpu.roll(outer, LANES - 32, axis=1)
    for block in range(SIDE):
        message[block, :, LANES:] = jnp.where(lane < 32, sums[block], pltpu.roll(sums[block + 2], 32, axis=1))
    near[:, :LANES] = nodes[here]
    near[:, LANES:] = jnp.where(lane < 32, spots[here], pltpu.roll(spots[here + 2], 32, axis=1))


def swept_kernel(received, near, cells, motion_out, swept_out):
    total = received[0]
    for i in range(1, SIDE):
        total = total + received[i]
    top = [total[i : i + 1] for i in range(3)]
    turn = [total[i : i + 1] for i in range(3, 6)]
    spot = [near[i : i + 1, :] for i in range(5, 8)]
    turned = cross3(turn, spot)
    motion = [(top[i] + turned[i]) / total[6:7] for i in range(3)]
    motion_out[...] = jnp.concatenate([m[:, :LANES] for m in motion], axis=0)
    table = jnp.concatenate(spot + motion + [jnp.zeros_like(spot[0])] * 2, axis=0)
    own, lent = table[:, :LANES], table[:, LANES:]
    count = cells.shape[1]
    for group in range(count // LANES):
        corner = []
        for a in range(4):
            index = cells[a : a + 1, group * LANES : (group + 1) * LANES]
            inside = (index >= 32) & (index < 160)
            from_own = pick_lanes(own, jnp.where(inside, index - 32, 0))
            from_lent = pick_lanes(lent, jnp.where(inside, 0, jnp.where(index < 32, index, index - 128)))
            corner.append(jnp.where(jnp.broadcast_to(inside, own.shape), from_own, from_lent))
        move = [[c[3 + i : 4 + i] for i in range(3)] for c in corner]
        half = [[c[i : i + 1] + 0.5 * c[3 + i : 4 + i] for i in range(3)] for c in corner]
        result = jnp.zeros((1, LANES), F32)
        for p, q, r in ((1, 2, 3), (0, 3, 2), (0, 1, 3), (0, 2, 1)):
            one = [half[q][i] - half[p][i] for i in range(3)]
            two = [half[r][i] - half[p][i] for i in range(3)]
            normal = cross3(one, two)
            for i in range(3):
                average = (move[p][i] + move[q][i] + move[r][i]) / 3.0
                result = result + average * (0.5 * normal[i])
        swept_out[group : group + 1, :] = result


def shards(points, surface, displacement, rotation, halo_index, connectivity):
    width = surface.shape[1]
    nodes = points.shape[1]
    lend = halo_index.shape[0]
    message, own, lent = pl.pallas_call(
        prepare_kernel,
        out_shape=(
            jax.ShapeDtypeStruct((SIDE, 8, width + LANES), F32),
            jax.ShapeDtypeStruct((SIDE, 8, LANES), F32),
            jax.ShapeDtypeStruct((8, LANES), F32),
        ),
        scratch_shapes=[pltpu.VMEM((8, LANES), jnp.int32)],
    )(points, surface, displacement, rotation, halo_index.reshape(1, lend))
    total_surface = SIDE * width
    early = lax.axis_index("zh") == 0

    def ahead():
        beside = lax.all_to_all(own, "y", 0, 0)
        near_surfaces = lax.all_to_all(message[: SIDE // 2], "zl", 0, 0)
        return pl.pallas_call(
            early_kernel,
            out_shape=jax.ShapeDtypeStruct((SIDE, 24, nodes), F32),
            scratch_shapes=[
                pltpu.VMEM((total_surface // 2, LANES), BF16),
                pltpu.VMEM((16, total_surface // 2), BF16),
                pltpu.VMEM((LANES, SIDE * LANES), BF16),
                pltpu.VMEM((16, SIDE * LANES), F32),
            ],
            compiler_params=pltpu.CompilerParams(vmem_limit_bytes=40 << 20),
            cost_estimate=pl.CostEstimate(flops=15 * 10**9, bytes_accessed=1 << 20, transcendentals=4 << 20),
        )(beside, near_surfaces)

    before = lax.cond(early, ahead, lambda: jnp.zeros((SIDE, 24, nodes), F32))
    message, lent, before = lax.optimization_barrier((message, lent, before))
    rows = lax.axis_size("vol") * SIDE
    ends = []
    for row in range(rows):
        after = (row + 1) % rows
        ends += [(row * SIDE + SIDE - 1, after * SIDE + SIDE - 1), (after * SIDE, row * SIDE)]
    outer = lax.ppermute(lent, ("vol", "zh", "zl", "y"), ends)
    surfaces = lax.all_to_all(message, ("zh", "zl"), 0, 0)
    surfaces, ready = lax.optimization_barrier((surfaces, own + outer))
    around = lax.all_to_all(ready, "y", 0, 0)
    flag = early.astype(jnp.int32)
    vmem = pl.BlockSpec(memory_space=pltpu.VMEM)
    smem = pl.BlockSpec(memory_space=pltpu.SMEM)
    right, terms, known = pl.pallas_call(
        own_kernel,
        out_shape=(
            jax.ShapeDtypeStruct((total_surface, LANES), BF16),
            jax.ShapeDtypeStruct((16, total_surface), BF16),
            jax.ShapeDtypeStruct((8, SIDE * LANES), F32),
        ),
        in_specs=[smem, vmem, vmem, vmem],
        out_specs=(vmem, vmem, vmem),
        scratch_shapes=[pltpu.VMEM((LANES, SIDE * LANES), BF16), pltpu.VMEM((16, SIDE * LANES), F32)],
        compiler_params=pltpu.CompilerParams(vmem_limit_bytes=40 << 20),
        cost_estimate=pl.CostEstimate(flops=15 * 10**9, bytes_accessed=3 << 20, transcendentals=4 << 20),
    )(flag.reshape(1), points, surfaces, before)
    place = jnp.stack([lax.axis_index("y").astype(jnp.int32), flag])
    partial, near = pl.pallas_call(
        sums_kernel,
        out_shape=(
            jax.ShapeDtypeStruct((SIDE, 8, 2 * LANES), F32),
            jax.ShapeDtypeStruct((8, 2 * LANES), F32),
        ),
        in_specs=[smem, vmem, vmem, vmem, vmem],
        out_specs=(vmem, vmem),
        scratch_shapes=[
            pltpu.VMEM((LANES, SIDE * LANES), BF16),
            pltpu.VMEM((16, SIDE * LANES), F32),
            pltpu.VMEM((SIDE + 2, 8, LANES), F32),
            pltpu.VMEM((SIDE + 2, 8, LANES), F32),
        ],
        compiler_params=pltpu.CompilerParams(vmem_limit_bytes=40 << 20),
        cost_estimate=pl.CostEstimate(flops=30 * 10**9, bytes_accessed=3 << 20, transcendentals=8 << 20),
    )(place, around, right, terms, known)
    received = lax.all_to_all(partial, "y", 0, 0)
    count = connectivity.shape[1]
    motion, swept = pl.pallas_call(
        swept_kernel,
        out_shape=(
            jax.ShapeDtypeStruct((3, nodes), F32),
            jax.ShapeDtypeStruct((count // LANES, LANES), F32),
        ),
        compiler_params=pltpu.CompilerParams(vmem_limit_bytes=8 << 20),
    )(received, near, connectivity)
    return motion, swept.reshape(count)


def solution(mesh):
    split = Mesh(mesh.devices.reshape(mesh.devices.shape[0], 2, SIDE // 2, SIDE), ("vol", "zh", "zl", "y"))
    nodes = ("vol", "zh", "zl", "y")
    surface = P(None, ("zh", "zl", "y"))
    in_specs = (P(None, nodes), surface, surface, surface, P(nodes), P(None, nodes))
    out_specs = (P(None, nodes), P(nodes))
    return jax.shard_map(shards, mesh=split, in_specs=in_specs, out_specs=out_specs, check_vma=False)
```

```python
import jax
import jax.numpy as jnp
from jax import lax
from jax.experimental import pallas as pl
from jax.experimental.pallas import tpu as pltpu
from jax.sharding import Mesh
from jax.sharding import PartitionSpec as P

SOFTENING = 0.01
F32 = jnp.float32
BF16 = jnp.bfloat16
SIDE = 8
LANES = 128
OWN_STEP = 8192
SURF_STEP = 4096


def rows_of(shape):
    return lax.broadcasted_iota(jnp.int32, shape, 0)


def lanes_of(shape):
    return lax.broadcasted_iota(jnp.int32, shape, 1)


def cross3(a, b):
    return (
        a[1] * b[2] - a[2] * b[1],
        a[2] * b[0] - a[0] * b[2],
        a[0] * b[1] - a[1] * b[0],
    )


def in_three(value):
    high = value.astype(BF16).astype(F32)
    rest = value - high
    middle = rest.astype(BF16).astype(F32)
    return high, middle, rest - middle


def pick_lanes(table, index):
    spread = jnp.broadcast_to(index, table.shape)
    return jnp.take_along_axis(table, spread, axis=1, mode="promise_in_bounds")


def prepare_kernel(points, surface, displacement, rotation, halo, message, own, lent, index):
    at = [surface[i : i + 1, :] for i in range(3)]
    turn = [rotation[i : i + 1, :] for i in range(3)]
    rotated = cross3(turn, at)
    term = [displacement[i : i + 1, :] - rotated[i] for i in range(3)]
    body = jnp.concatenate(term + turn[:2] + at, axis=0)
    last = jnp.concatenate([turn[2][:, i * LANES : (i + 1) * LANES] for i in range(SIDE)], axis=0)
    whole = jnp.concatenate([body, last], axis=1)
    for i in range(SIDE):
        message[i] = whole
    index[...] = jnp.zeros_like(index)
    index[0:1, 0 : halo.shape[1]] = halo[...]
    place = index[0:1, :]
    mine = jnp.concatenate(
        [jnp.zeros((3, LANES), F32), place.astype(F32), jnp.zeros((1, LANES), F32), points[...]], axis=0
    )
    for i in range(SIDE):
        own[i] = mine
    table = jnp.concatenate([points[...], jnp.zeros((5, LANES), F32)], axis=0)
    lent[...] = jnp.where(rows_of(table.shape) < 3, pick_lanes(table, place), 0.0)


def node_side(value):
    row = rows_of(value.shape)
    square = value[5:6] * value[5:6] + value[6:7] * value[6:7] + value[7:8] * value[7:8] + SOFTENING
    side = jnp.where(row >= 5, -2.0 * value, jnp.where(row == 3, 1.0, jnp.where(row == 4, square, 0.0)))
    high, middle, low = in_three(side)
    stack = [high, high, high, middle, middle, low, middle, low] + [jnp.zeros_like(high)] * 8
    return jnp.concatenate(stack, axis=0).astype(BF16)


def surface_side(value):
    row = rows_of(value.shape)
    square = value[5:6] * value[5:6] + value[6:7] * value[6:7] + value[7:8] * value[7:8]
    side = jnp.where(row >= 5, value, jnp.where(row == 3, square, jnp.where(row == 4, 1.0, 0.0)))
    high, middle, low = in_three(side)
    stack = [high, middle, low, high, middle, high, low, middle] + [jnp.zeros_like(high)] * 8
    return jnp.concatenate(stack, axis=0).T.astype(BF16)


def add_sums(right, terms, left, total, surf_step):
    def step(i, carry):
        s = pl.multiple_of(i * surf_step, LANES)
        spread = jnp.dot(right[pl.ds(s, surf_step), :], left[...], preferred_element_type=F32)
        inverse = lax.rsqrt(spread)
        weight = inverse * inverse * inverse
        high = weight.astype(BF16)
        low = (weight - high.astype(F32)).astype(BF16)
        term = terms[:, pl.ds(s, surf_step)]
        total[...] += jnp.dot(term, high, preferred_element_type=F32) + jnp.dot(
            term, low, preferred_element_type=F32
        )
        return carry

    total[...] = jnp.zeros_like(total)
    lax.fori_loop(0, right.shape[0] // surf_step, step, 0)


def own_kernel(points, surface, right, terms, sums, left, total):
    width = surface.shape[2] - LANES
    line = rows_of((SIDE, width))
    for part in range(SIDE):
        value = surface[part][:, :width]
        tail = surface[part][:, width:]
        tail = jnp.concatenate([tail[i : i + 1] for i in range(SIDE)], axis=1)
        right[part * width : (part + 1) * width, :] = surface_side(value)
        term = jnp.where(line < 5, value, jnp.where(line == 5, tail, jnp.where(line == 6, 1.0, 0.0)))
        high, middle, _ = in_three(term)
        terms[:, part * width : (part + 1) * width] = jnp.concatenate([high, middle], axis=0).astype(BF16)
    left[...] = node_side(jnp.concatenate([jnp.zeros((5, LANES), F32), points[...]], axis=0))
    add_sums(right, terms, left, total, OWN_STEP)
    sums[...] = total[:SIDE] + total[SIDE:]


def sums_kernel(place, nodes, right, terms, own_sums, message, near, left, total, sums, spots):
    lane = lanes_of((SIDE, LANES))
    here = place[0]
    outer = jnp.where(lane < 32, nodes[0], pltpu.roll(nodes[1], 32, axis=1))
    outer = pltpu.roll(outer, 5, axis=0)
    for k in range(SIDE):
        value = nodes[(here + k + 1) % SIDE] if k < SIDE - 1 else outer
        left[:, k * LANES : (k + 1) * LANES] = node_side(value)
    add_sums(right, terms, left, total, SURF_STEP)
    whole = total[:SIDE] + total[SIDE:]

    def keep(block, value):
        message[block, :, :LANES] = value
        index = nodes[block][3:4].astype(jnp.int32)
        sums[block + 1] = pick_lanes(value, index)
        spots[block + 1] = pick_lanes(nodes[block], index)

    keep(here, own_sums[...])
    for k in range(SIDE - 1):
        keep((here + k + 1) % SIDE, whole[:, k * LANES : (k + 1) * LANES])
    value = whole[:, (SIDE - 1) * LANES :]
    sums[0] = value
    sums[SIDE + 1] = pltpu.roll(value, LANES - 32, axis=1)
    spots[0] = outer
    spots[SIDE + 1] = pltpu.roll(outer, LANES - 32, axis=1)
    for block in range(SIDE):
        message[block, :, LANES:] = jnp.where(lane < 32, sums[block], pltpu.roll(sums[block + 2], 32, axis=1))
    near[:, :LANES] = nodes[here]
    near[:, LANES:] = jnp.where(lane < 32, spots[here], pltpu.roll(spots[here + 2], 32, axis=1))


def swept_kernel(received, near, cells, motion_out, swept_out):
    total = received[0]
    for i in range(1, SIDE):
        total = total + received[i]
    top = [total[i : i + 1] for i in range(3)]
    turn = [total[i : i + 1] for i in range(3, 6)]
    spot = [near[i : i + 1, :] for i in range(5, 8)]
    turned = cross3(turn, spot)
    motion = [(top[i] + turned[i]) / total[6:7] for i in range(3)]
    motion_out[...] = jnp.concatenate([m[:, :LANES] for m in motion], axis=0)
    table = jnp.concatenate(spot + motion + [jnp.zeros_like(spot[0])] * 2, axis=0)
    own, lent = table[:, :LANES], table[:, LANES:]
    count = cells.shape[1]
    for group in range(count // LANES):
        corner = []
        for a in range(4):
            index = cells[a : a + 1, group * LANES : (group + 1) * LANES]
            inside = (index >= 32) & (index < 160)
            from_own = pick_lanes(own, jnp.where(inside, index - 32, 0))
            from_lent = pick_lanes(lent, jnp.where(inside, 0, jnp.where(index < 32, index, index - 128)))
            corner.append(jnp.where(jnp.broadcast_to(inside, own.shape), from_own, from_lent))
        move = [[c[3 + i : 4 + i] for i in range(3)] for c in corner]
        half = [[c[i : i + 1] + 0.5 * c[3 + i : 4 + i] for i in range(3)] for c in corner]
        result = jnp.zeros((1, LANES), F32)
        for p, q, r in ((1, 2, 3), (0, 3, 2), (0, 1, 3), (0, 2, 1)):
            one = [half[q][i] - half[p][i] for i in range(3)]
            two = [half[r][i] - half[p][i] for i in range(3)]
            normal = cross3(one, two)
            for i in range(3):
                average = (move[p][i] + move[q][i] + move[r][i]) / 3.0
                result = result + average * (0.5 * normal[i])
        swept_out[group : group + 1, :] = result


def shards(points, surface, displacement, rotation, halo_index, connectivity):
    width = surface.shape[1]
    nodes = points.shape[1]
    lend = halo_index.shape[0]
    message, own, lent = pl.pallas_call(
        prepare_kernel,
        out_shape=(
            jax.ShapeDtypeStruct((SIDE, 8, width + LANES), F32),
            jax.ShapeDtypeStruct((SIDE, 8, LANES), F32),
            jax.ShapeDtypeStruct((8, LANES), F32),
        ),
        scratch_shapes=[pltpu.VMEM((8, LANES), jnp.int32)],
        cost_estimate=pl.CostEstimate(flops=3 * 10**9, bytes_accessed=8 << 20, transcendentals=0),
    )(points, surface, displacement, rotation, halo_index.reshape(1, lend))
    rows = lax.axis_size("vol") * SIDE
    ends = []
    for row in range(rows):
        after = (row + 1) % rows
        ends += [(row * SIDE + SIDE - 1, after * SIDE), (after * SIDE, row * SIDE + 1)]
    outer = lax.ppermute(lent, ("vol", "z", "y"), ends)
    surfaces = lax.all_to_all(message, "z", 0, 0)
    surfaces, ready = lax.optimization_barrier((surfaces, own + outer))
    around = lax.all_to_all(ready, "y", 0, 0)
    total_surface = SIDE * width
    right, terms, own_sums = pl.pallas_call(
        own_kernel,
        out_shape=(
            jax.ShapeDtypeStruct((total_surface, LANES), BF16),
            jax.ShapeDtypeStruct((16, total_surface), BF16),
            jax.ShapeDtypeStruct((8, LANES), F32),
        ),
        scratch_shapes=[pltpu.VMEM((LANES, LANES), BF16), pltpu.VMEM((16, LANES), F32)],
        compiler_params=pltpu.CompilerParams(vmem_limit_bytes=24 << 20),
        cost_estimate=pl.CostEstimate(flops=5 * 10**9, bytes_accessed=3 << 20, transcendentals=1 << 20),
    )(points, surfaces)
    place = lax.axis_index("y").astype(jnp.int32).reshape(1)
    vmem = pl.BlockSpec(memory_space=pltpu.VMEM)
    partial, near = pl.pallas_call(
        sums_kernel,
        out_shape=(
            jax.ShapeDtypeStruct((SIDE, 8, 2 * LANES), F32),
            jax.ShapeDtypeStruct((8, 2 * LANES), F32),
        ),
        in_specs=[pl.BlockSpec(memory_space=pltpu.SMEM), vmem, vmem, vmem, vmem],
        out_specs=(vmem, vmem),
        scratch_shapes=[
            pltpu.VMEM((LANES, SIDE * LANES), BF16),
            pltpu.VMEM((16, SIDE * LANES), F32),
            pltpu.VMEM((SIDE + 2, 8, LANES), F32),
            pltpu.VMEM((SIDE + 2, 8, LANES), F32),
        ],
        compiler_params=pltpu.CompilerParams(vmem_limit_bytes=40 << 20),
        cost_estimate=pl.CostEstimate(flops=30 * 10**9, bytes_accessed=3 << 20, transcendentals=8 << 20),
    )(place, around, right, terms, own_sums)
    received = lax.all_to_all(partial, "y", 0, 0)
    count = connectivity.shape[1]
    motion, swept = pl.pallas_call(
        swept_kernel,
        out_shape=(
            jax.ShapeDtypeStruct((3, nodes), F32),
            jax.ShapeDtypeStruct((count // LANES, LANES), F32),
        ),
        compiler_params=pltpu.CompilerParams(vmem_limit_bytes=8 << 20),
    )(received, near, connectivity)
    return motion, swept.reshape(count)


def solution(mesh):
    split = Mesh(mesh.devices.reshape(mesh.devices.shape[0], SIDE, SIDE), ("vol", "z", "y"))
    nodes = ("vol", "z", "y")
    surface = P(None, ("z", "y"))
    in_specs = (P(None, nodes), surface, surface, surface, P(nodes), P(None, nodes))
    out_specs = (P(None, nodes), P(nodes))
    return jax.shard_map(shards, mesh=split, in_specs=in_specs, out_specs=out_specs, check_vma=False)
```

```python
import jax
import jax.numpy as jnp
from jax import lax
from jax.experimental import pallas as pl
from jax.experimental.pallas import tpu as pltpu
from jax.sharding import Mesh
from jax.sharding import PartitionSpec as P

SOFTENING = 0.01
F32 = jnp.float32
BF16 = jnp.bfloat16
SIDE = 8
LANES = 128
OWN_STEP = 8192
SURF_STEP = 4096


def rows_of(shape):
    return lax.broadcasted_iota(jnp.int32, shape, 0)


def lanes_of(shape):
    return lax.broadcasted_iota(jnp.int32, shape, 1)


def cross3(a, b):
    return (
        a[1] * b[2] - a[2] * b[1],
        a[2] * b[0] - a[0] * b[2],
        a[0] * b[1] - a[1] * b[0],
    )


def in_three(value):
    high = value.astype(BF16).astype(F32)
    rest = value - high
    middle = rest.astype(BF16).astype(F32)
    return high, middle, rest - middle


def pick_lanes(table, index):
    spread = jnp.broadcast_to(index, table.shape)
    return jnp.take_along_axis(table, spread, axis=1, mode="promise_in_bounds")


def prepare_kernel(points, surface, displacement, rotation, halo, message, own, lent, index):
    at = [surface[i : i + 1, :] for i in range(3)]
    turn = [rotation[i : i + 1, :] for i in range(3)]
    rotated = cross3(turn, at)
    term = [displacement[i : i + 1, :] - rotated[i] for i in range(3)]
    body = jnp.concatenate(term + turn[:2] + at, axis=0)
    last = jnp.concatenate([turn[2][:, i * LANES : (i + 1) * LANES] for i in range(SIDE)], axis=0)
    whole = jnp.concatenate([body, last], axis=1)
    for i in range(SIDE):
        message[i] = whole
    index[...] = jnp.zeros_like(index)
    index[0:1, 0 : halo.shape[1]] = halo[...]
    place = index[0:1, :]
    mine = jnp.concatenate(
        [jnp.zeros((3, LANES), F32), place.astype(F32), jnp.zeros((1, LANES), F32), points[...]], axis=0
    )
    for i in range(SIDE):
        own[i] = mine
    table = jnp.concatenate([points[...], jnp.zeros((5, LANES), F32)], axis=0)
    lent[...] = jnp.where(rows_of(table.shape) < 3, pick_lanes(table, place), 0.0)


def node_side(value):
    row = rows_of(value.shape)
    square = value[5:6] * value[5:6] + value[6:7] * value[6:7] + value[7:8] * value[7:8] + SOFTENING
    side = jnp.where(row >= 5, -2.0 * value, jnp.where(row == 3, 1.0, jnp.where(row == 4, square, 0.0)))
    high, middle, low = in_three(side)
    stack = [high, high, high, middle, middle, low, middle, low] + [jnp.zeros_like(high)] * 8
    return jnp.concatenate(stack, axis=0).astype(BF16)


def surface_side(value):
    row = rows_of(value.shape)
    square = value[5:6] * value[5:6] + value[6:7] * value[6:7] + value[7:8] * value[7:8]
    side = jnp.where(row >= 5, value, jnp.where(row == 3, square, jnp.where(row == 4, 1.0, 0.0)))
    high, middle, low = in_three(side)
    stack = [high, middle, low, high, middle, high, low, middle] + [jnp.zeros_like(high)] * 8
    return jnp.concatenate(stack, axis=0).T.astype(BF16)


def add_sums(right, terms, left, total, surf_step):
    def step(i, carry):
        s = pl.multiple_of(i * surf_step, LANES)
        spread = jnp.dot(right[pl.ds(s, surf_step), :], left[...], preferred_element_type=F32)
        inverse = lax.rsqrt(spread)
        weight = inverse * inverse * inverse
        high = weight.astype(BF16)
        low = (weight - high.astype(F32)).astype(BF16)
        term = terms[:, pl.ds(s, surf_step)]
        total[...] += jnp.dot(term, high, preferred_element_type=F32) + jnp.dot(
            term, low, preferred_element_type=F32
        )
        return carry

    total[...] = jnp.zeros_like(total)
    lax.fori_loop(0, right.shape[0] // surf_step, step, 0)


def own_kernel(points, surface, right, terms, sums, left, total):
    width = surface.shape[2] - LANES
    line = rows_of((SIDE, width))
    for part in range(SIDE):
        value = surface[part][:, :width]
        tail = surface[part][:, width:]
        tail = jnp.concatenate([tail[i : i + 1] for i in range(SIDE)], axis=1)
        right[part * width : (part + 1) * width, :] = surface_side(value)
        term = jnp.where(line < 5, value, jnp.where(line == 5, tail, jnp.where(line == 6, 1.0, 0.0)))
        high, middle, _ = in_three(term)
        terms[:, part * width : (part + 1) * width] = jnp.concatenate([high, middle], axis=0).astype(BF16)
    left[...] = node_side(jnp.concatenate([jnp.zeros((5, LANES), F32), points[...]], axis=0))
    add_sums(right, terms, left, total, OWN_STEP)
    sums[...] = total[:SIDE] + total[SIDE:]


def sums_kernel(place, nodes, right, terms, own_sums, message, near, left, total, sums, spots):
    lane = lanes_of((SIDE, LANES))
    here = place[0]
    outer = jnp.where(lane < 32, nodes[0], pltpu.roll(nodes[1], 32, axis=1))
    outer = pltpu.roll(outer, 5, axis=0)
    for k in range(SIDE):
        value = nodes[(here + k + 1) % SIDE] if k < SIDE - 1 else outer
        left[:, k * LANES : (k + 1) * LANES] = node_side(value)
    add_sums(right, terms, left, total, SURF_STEP)
    whole = total[:SIDE] + total[SIDE:]

    def keep(block, value):
        message[block, 0] = value[:4]
        message[block, 1] = value[4:]
        index = nodes[block][3:4].astype(jnp.int32)
        sums[block + 1] = pick_lanes(value, index)
        spots[block + 1] = pick_lanes(nodes[block], index)

    keep(here, own_sums[...])
    for k in range(SIDE - 1):
        keep((here + k + 1) % SIDE, whole[:, k * LANES : (k + 1) * LANES])
    value = whole[:, (SIDE - 1) * LANES :]
    sums[0] = value
    sums[SIDE + 1] = pltpu.roll(value, LANES - 32, axis=1)
    spots[0] = outer
    spots[SIDE + 1] = pltpu.roll(outer, LANES - 32, axis=1)
    for block in range(SIDE):
        lent = jnp.where(lane < 32, sums[block], pltpu.roll(sums[block + 2], 32, axis=1))
        right_half = pltpu.roll(pltpu.roll(lent, 4, axis=0), 64, axis=1)
        message[block, 2] = jnp.where(lane < 64, lent, right_half)[:4]
    near[:, :LANES] = nodes[here]
    near[:, LANES:] = jnp.where(lane < 32, spots[here], pltpu.roll(spots[here + 2], 32, axis=1))


def swept_kernel(received, near, cells, motion_out, swept_out):
    whole = received[0]
    for i in range(1, SIDE):
        whole = whole + received[i]
    packed = whole[2]
    total = jnp.concatenate(
        [
            jnp.concatenate([whole[0], whole[1]], axis=0),
            jnp.concatenate([packed, pltpu.roll(packed, 64, axis=1)], axis=0),
        ],
        axis=1,
    )
    top = [total[i : i + 1] for i in range(3)]
    turn = [total[i : i + 1] for i in range(3, 6)]
    spot = [near[i : i + 1, :] for i in range(5, 8)]
    turned = cross3(turn, spot)
    motion = [(top[i] + turned[i]) / total[6:7] for i in range(3)]
    motion_out[...] = jnp.concatenate([m[:, :LANES] for m in motion], axis=0)
    table = jnp.concatenate(spot + motion + [jnp.zeros_like(spot[0])] * 2, axis=0)
    own, lent = table[:, :LANES], table[:, LANES:]
    count = cells.shape[1]
    for group in range(count // LANES):
        corner = []
        for a in range(4):
            index = cells[a : a + 1, group * LANES : (group + 1) * LANES]
            inside = (index >= 32) & (index < 160)
            from_own = pick_lanes(own, jnp.where(inside, index - 32, 0))
            from_lent = pick_lanes(lent, jnp.where(inside, 0, jnp.where(index < 32, index, index - 128)))
            corner.append(jnp.where(jnp.broadcast_to(inside, own.shape), from_own, from_lent))
        move = [[c[3 + i : 4 + i] for i in range(3)] for c in corner]
        half = [[c[i : i + 1] + 0.5 * c[3 + i : 4 + i] for i in range(3)] for c in corner]
        result = jnp.zeros((1, LANES), F32)
        for p, q, r in ((1, 2, 3), (0, 3, 2), (0, 1, 3), (0, 2, 1)):
            one = [half[q][i] - half[p][i] for i in range(3)]
            two = [half[r][i] - half[p][i] for i in range(3)]
            normal = cross3(one, two)
            for i in range(3):
                average = (move[p][i] + move[q][i] + move[r][i]) / 3.0
                result = result + average * (0.5 * normal[i])
        swept_out[group : group + 1, :] = result


def shards(points, surface, displacement, rotation, halo_index, connectivity):
    width = surface.shape[1]
    nodes = points.shape[1]
    lend = halo_index.shape[0]
    message, own, lent = pl.pallas_call(
        prepare_kernel,
        out_shape=(
            jax.ShapeDtypeStruct((SIDE, 8, width + LANES), F32),
            jax.ShapeDtypeStruct((SIDE, 8, LANES), F32),
            jax.ShapeDtypeStruct((8, LANES), F32),
        ),
        scratch_shapes=[pltpu.VMEM((8, LANES), jnp.int32)],
        cost_estimate=pl.CostEstimate(flops=3 * 10**9, bytes_accessed=8 << 20, transcendentals=0),
    )(points, surface, displacement, rotation, halo_index.reshape(1, lend))
    rows = lax.axis_size("vol") * SIDE
    ends = []
    for row in range(rows):
        after = (row + 1) % rows
        ends += [(row * SIDE + SIDE - 1, after * SIDE), (after * SIDE, row * SIDE + 1)]
    outer = lax.ppermute(lent, ("vol", "z", "y"), ends)
    surfaces = lax.all_to_all(message, "z", 0, 0)
    surfaces, ready = lax.optimization_barrier((surfaces, own + outer))
    around = lax.all_to_all(ready, "y", 0, 0)
    total_surface = SIDE * width
    right, terms, own_sums = pl.pallas_call(
        own_kernel,
        out_shape=(
            jax.ShapeDtypeStruct((total_surface, LANES), BF16),
            jax.ShapeDtypeStruct((16, total_surface), BF16),
            jax.ShapeDtypeStruct((8, LANES), F32),
        ),
        scratch_shapes=[pltpu.VMEM((LANES, LANES), BF16), pltpu.VMEM((16, LANES), F32)],
        compiler_params=pltpu.CompilerParams(vmem_limit_bytes=24 << 20),
        cost_estimate=pl.CostEstimate(flops=5 * 10**9, bytes_accessed=3 << 20, transcendentals=1 << 20),
    )(points, surfaces)
    place = lax.axis_index("y").astype(jnp.int32).reshape(1)
    vmem = pl.BlockSpec(memory_space=pltpu.VMEM)
    partial, near = pl.pallas_call(
        sums_kernel,
        out_shape=(
            jax.ShapeDtypeStruct((SIDE, 3, 4, LANES), F32),
            jax.ShapeDtypeStruct((8, 2 * LANES), F32),
        ),
        in_specs=[pl.BlockSpec(memory_space=pltpu.SMEM), vmem, vmem, vmem, vmem],
        out_specs=(vmem, vmem),
        scratch_shapes=[
            pltpu.VMEM((LANES, SIDE * LANES), BF16),
            pltpu.VMEM((16, SIDE * LANES), F32),
            pltpu.VMEM((SIDE + 2, 8, LANES), F32),
            pltpu.VMEM((SIDE + 2, 8, LANES), F32),
        ],
        compiler_params=pltpu.CompilerParams(vmem_limit_bytes=40 << 20),
        cost_estimate=pl.CostEstimate(flops=30 * 10**9, bytes_accessed=3 << 20, transcendentals=8 << 20),
    )(place, around, right, terms, own_sums)
    received = lax.all_to_all(partial, "y", 0, 0)
    count = connectivity.shape[1]
    motion, swept = pl.pallas_call(
        swept_kernel,
        out_shape=(
            jax.ShapeDtypeStruct((3, nodes), F32),
            jax.ShapeDtypeStruct((count // LANES, LANES), F32),
        ),
        compiler_params=pltpu.CompilerParams(vmem_limit_bytes=8 << 20),
    )(received, near, connectivity)
    return motion, swept.reshape(count)


def solution(mesh):
    split = Mesh(mesh.devices.reshape(mesh.devices.shape[0], SIDE, SIDE), ("vol", "z", "y"))
    nodes = ("vol", "z", "y")
    surface = P(None, ("z", "y"))
    in_specs = (P(None, nodes), surface, surface, surface, P(nodes), P(None, nodes))
    out_specs = (P(None, nodes), P(nodes))
    return jax.shard_map(shards, mesh=split, in_specs=in_specs, out_specs=out_specs, check_vma=False)
```
